256 devices in a mesh: seq: 32 (over y, x, core), tensor: 8 (over z).
Axes of the slice: x: 4, y: 4, z: 8, core: 2. Of those that a mesh axis runs over, the one named last changes fastest.
Arguments:
- queries: bfloat16 [4096, 8192], P('seq', 'tensor'), may hold values from -6 to 6
- key_vectors: bfloat16 [4096, 8192], P('seq', 'tensor'), may hold values from -6 to 6
- value_rows: bfloat16 [4096, 8192], P('seq', 'tensor'), may hold values from -6 to 6
- gate_logits: bfloat16 [4096, 8192], P('seq', 'tensor'), may hold values from -6 to 6
- log_decay: float32 [4096, 64], P('seq', 'tensor'), may hold values from -0.73 to 0, as said below
- initial_state: float32 [64, 128, 128], P('tensor'), may hold values from -192 to 192
- norm_gain: float32 [8192], P('tensor'), may hold values from 0.25 to 1.75
- out_weight: bfloat16 [8192, 6144], P('tensor', 'seq'), may hold values from -0.0625 to 0.0625
Outputs:
- mixed: float32 [4096, 6144], P('seq', 'tensor')
The draws below stay inside these ranges and needn't reach their ends.
Inputs may be any that keep to these rules, and one draw needn't show every extreme that they name: `log_decay`: every entry is negative.
All inputs are finite; a program needn't handle non-finite values.
Results may differ from the reference program's by a relative error of at most 0.0075.
Values may be sent and summed in bfloat16 or wider, within the bound.
No kernel may reach another device: no remote copies, remote signals or barrier semaphores. Data moves between devices by JAX's collectives and lax.ppermute only.
A program may use at most 128 MiB of HBM per device.

```python
import jax
import jax.numpy as jnp
from jax import lax

D = 6144
HEADS = 64
DK = 128
TOK_DEV = 128
TOKENS = 4096
HD = 8192


def draw_log_decay(key, part):
    kind_key, slow_key, fast_key, place_key, loss_key = jax.random.split(key, 5)
    fast_share = 0.5
    is_fast = jax.random.uniform(kind_key, (HEADS,), jnp.float32) < fast_share
    slow_rate = jnp.exp(jax.random.uniform(slow_key, (HEADS,), jnp.float32, jnp.log(0.01), jnp.log(0.2))) / TOKENS
    fast_rate = jnp.exp(jax.random.uniform(fast_key, (HEADS,), jnp.float32, jnp.log(1.0 / 50.0), jnp.log(1.0 / 30.0)))
    fading_factor = jnp.where(is_fast, fast_rate, slow_rate)
    places = jax.random.randint(place_key, (3,), 0, TOKENS)
    token_positions = jnp.arange(TOKENS, dtype=jnp.int32)
    attenuated_matrix_items = jnp.any(token_positions[:, None] == places[None, :], axis=1)
    objective_samples = jax.random.uniform(loss_key, (TOKENS, HEADS), jnp.float32, 0.2, 0.5)
    sequence_segments = jnp.where(attenuated_matrix_items[:, None], jnp.log(1.0 - objective_samples), 0.0)
    return (sequence_segments - fading_factor[None, :]).astype(jnp.float32)


def block_levels(rng, shape, cuts, low, largest):
    gain = 1.0
    for dim, shards_of in cuts:
        steps = jax.random.uniform(jax.random.fold_in(jax.random.fold_in(rng, 6), dim), (shards_of,), jnp.float32, low / len(cuts), largest / len(cuts))
        gain = gain * jnp.repeat(jnp.exp(steps), shape[dim] // shards_of).reshape((-1,) + (1,) * (len(shape) - 1 - dim))
    return gain


def centred(key, extent, deviation, reach, cuts=(), kind=jnp.bfloat16):
    level = block_levels(key, extent, cuts, -0.22, 0.18) if cuts else 1.0
    values = jax.random.normal(key, extent, jnp.float32) * deviation * level
    return jnp.minimum(jnp.maximum(values, -reach), reach).astype(kind)


def setup_inputs(seed: int = 0) -> dict:
    arg_keys = jax.random.split(jax.random.key(seed), 9)
    queries = centred(arg_keys[0], (TOKENS, HD), 1.0, 6.0, ((0, 32), (1, 8)))
    key_vectors = centred(arg_keys[1], (TOKENS, HD), 1.0, 6.0, ((0, 32), (1, 8)))
    value_rows = centred(arg_keys[2], (TOKENS, HD), 1.0, 6.0, ((0, 32), (1, 8)))
    gate_logits = centred(arg_keys[3], (TOKENS, HD), 1.5, 6.0, ((0, 32), (1, 8)))
    log_decay = draw_log_decay(jax.random.fold_in(arg_keys[8], 71), 0)
    initial_state = centred(arg_keys[5], (HEADS, DK, DK), (TOK_DEV // 4), 192.0, ((0, 8),), jnp.float32)
    norm_gain = jnp.clip(1.0 + 0.15 * jax.random.normal(arg_keys[6], (HD,), jnp.float32), 0.25, 1.75)
    out_weight = centred(arg_keys[7], (HD, D), HD ** -0.5, 0.0625, ((0, 8), (1, 32)))
    return {"queries": queries, "key_vectors": key_vectors, "value_rows": value_rows, "gate_logits": gate_logits, "log_decay": log_decay, "initial_state": initial_state, "norm_gain": norm_gain, "out_weight": out_weight}


HIGH = lax.Precision.HIGHEST

def block_attention_step(state, pieces):
    queries_b, keys_b, values_b, decay_b = pieces
    q_float = queries_b.astype(jnp.float32)
    keys_single_precise = keys_b.astype(jnp.float32)
    v_float = values_b.astype(jnp.float32)
    cumulative_memory = jnp.cumsum(decay_b, axis=0)
    total = cumulative_memory[-1]
    carried = jnp.exp(cumulative_memory)[:, :, None] * jnp.einsum('thd,hde->the', q_float, state, precision=HIGH)
    scores = jnp.einsum('thd,shd->hts', q_float, keys_single_precise, precision=HIGH)
    length = cumulative_memory.shape[0]
    lower = jnp.tril(jnp.ones((length, length), dtype=bool))[None]
    spread = cumulative_memory.T[:, :, None] - cumulative_memory.T[:, None, :]
    weights = jnp.where(lower, jnp.exp(jnp.where(lower, spread, 0.0)), 0.0)
    mixes = lax.optimization_barrier((scores * weights).astype(jnp.bfloat16)).astype(jnp.float32)
    local = jnp.einsum('hts,she->the', mixes, v_float, precision=HIGH)
    scaled = keys_single_precise * jnp.exp(total[None, :] - cumulative_memory)[:, :, None]
    new_state = jnp.exp(total)[:, None, None] * state + jnp.einsum('shd,she->hde', scaled, v_float, precision=HIGH)
    return (new_state, carried + local)

def normalize(attended, norm_gain, gate_logits):
    mean_square = lax.optimization_barrier(jnp.mean(attended * attended, axis=-1, keepdims=True))
    normalized_output = attended * lax.rsqrt(mean_square + 1e-05)
    flat = normalized_output.reshape(attended.shape[0], -1)
    gated = flat * norm_gain[None, :] * jax.nn.sigmoid(gate_logits.astype(jnp.float32))
    return gated.astype(jnp.bfloat16)

def reference(queries, key_vectors, value_rows, gate_logits, log_decay, initial_state, norm_gain, out_weight):
    block_len = min(512, TOKENS)
    block_count = TOKENS // block_len

    def shaped(array):
        return array.reshape(block_count, block_len, HEADS, DK)
    decay_blocks = log_decay.reshape(block_count, block_len, HEADS)
    final_state, outputs = lax.scan(block_attention_step, initial_state, (shaped(queries), shaped(key_vectors), shaped(value_rows), decay_blocks))
    attended = outputs.reshape(TOKENS, HEADS, DK)
    hidden = normalize(attended, norm_gain, gate_logits)
    return jnp.dot(hidden, out_weight, preferred_element_type=jnp.float32)
```

```python
import jax
import jax.numpy as jnp
from jax import lax
from jax.sharding import PartitionSpec as P

HIGH = lax.Precision.HIGHEST


def entering(array, axis, combine, identity):
    length, mine = (lax.axis_size(axis), lax.axis_index(axis))
    everything = jax.tree.map(lambda part: lax.all_gather(part, axis), array)
    start = jax.tree.map(
        lambda part, zero: jnp.broadcast_to(jnp.asarray(zero, part.dtype), part.shape),
        array,
        identity,
    )

    def hop(k, before):
        reached = k < mine
        new = combine(before, jax.tree.map(lambda part: part[k], everything))
        return jax.tree.map(lambda a, b: jnp.where(reached, a, b), new, before)

    return lax.fori_loop(0, length, hop, start)


def block_step(state, pieces):
    queries_b, keys_b, values_b, decay_b = pieces
    cumulative_memory = jnp.cumsum(decay_b, axis=0)
    total = cumulative_memory[-1]
    carried = jnp.exp(cumulative_memory)[:, :, None] * jnp.einsum(
        "thd,hde->the", queries_b.astype(jnp.float32), state, precision=HIGH
    )
    scores = jnp.einsum("thd,shd->hts", queries_b, keys_b, preferred_element_type=jnp.float32)
    length = cumulative_memory.shape[0]
    lower = jnp.tril(jnp.ones((length, length), dtype=bool))[None]
    spread = cumulative_memory.T[:, :, None] - cumulative_memory.T[:, None, :]
    weights = jnp.where(lower, jnp.exp(jnp.where(lower, spread, 0.0)), 0.0)
    mixes = (scores * weights).astype(jnp.bfloat16)
    local = jnp.einsum("hts,she->the", mixes, values_b, preferred_element_type=jnp.float32)
    scaled = keys_b.astype(jnp.float32) * jnp.exp(total[None, :] - cumulative_memory)[:, :, None]
    new_state = jnp.exp(total)[:, None, None] * state + jnp.einsum(
        "shd,she->hde", scaled, values_b.astype(jnp.float32), precision=HIGH
    )
    return (new_state, carried + local)


def normalize(attended, norm_gain, gate_logits):
    mean_square = jnp.mean(attended * attended, axis=-1, keepdims=True)
    normalized_output = attended * lax.rsqrt(mean_square + 1e-05)
    flat = normalized_output.reshape(attended.shape[0], -1)
    gated = flat * norm_gain[None, :] * jax.nn.sigmoid(gate_logits.astype(jnp.float32))
    return gated.astype(jnp.bfloat16)


def chain_link(earlier, later):
    return (earlier[0] * later[0], later[0][:, None, None] * earlier[1] + later[1])


def pack(rates, state):
    heads = state.shape[0]
    flat = state.reshape(heads, -1)
    lanes = jnp.broadcast_to(rates[:, None], (heads, 128))
    return jnp.concatenate([flat, lanes], axis=1)


def link_packed(earlier, later):
    width = later.shape[1] - 128
    later_rate = later[:, width:width + 1]
    state = later_rate * earlier[:, :width] + later[:, :width]
    rate = earlier[:, width:] * later[:, width:]
    return jnp.concatenate([state, rate], axis=1)


def carried_in(rates, state, initial_state):
    length, mine = (lax.axis_size("seq"), lax.axis_index("seq"))
    own = pack(rates, state)
    shifted = lax.ppermute(own, "seq", [(i, i + 1) for i in range(length - 1)])
    first = pack(jnp.ones_like(rates), initial_state)
    current = jnp.where(mine == 0, first, shifted)
    step = 1
    while step < length:
        earlier = lax.ppermute(current, "seq", [(i, i + step) for i in range(length - step)])
        current = jnp.where(mine >= step, link_packed(earlier, current), current)
        step *= 2
    width = current.shape[1] - 128
    return current[:, :width].reshape(state.shape)

def per_device(
    queries, key_vectors, value_rows, gate_logits, log_decay, initial_state, norm_gain, out_weight
):
    rows_here = queries.shape[0]
    head_count = log_decay.shape[1]
    head_dim = initial_state.shape[1]
    block_len = min(512, rows_here)
    block_count = rows_here // block_len

    def shaped(array):
        return array.reshape(block_count, block_len, head_count, head_dim)

    zero_state = jnp.zeros((head_count, head_dim, head_dim), jnp.float32)
    decay_blocks = log_decay.reshape(block_count, block_len, head_count)
    device_state, outputs = lax.scan(
        block_step,
        zero_state,
        (shaped(queries), shaped(key_vectors), shaped(value_rows), decay_blocks),
    )
    local_out = outputs.reshape(rows_here, head_count, head_dim)
    through = jnp.cumsum(log_decay, axis=0)
    shard_fading_rates = jnp.exp(through[-1])
    incoming = carried_in(shard_fading_rates, device_state, initial_state)
    query_float = queries.reshape(rows_here, head_count, head_dim).astype(jnp.float32)
    inherited = jnp.exp(through)[:, :, None] * jnp.einsum(
        "thd,hde->the", query_float, incoming, precision=HIGH
    )
    attended = local_out + inherited
    hidden = normalize(attended, norm_gain, gate_logits)
    terms = jnp.dot(
        hidden,
        lax.all_gather(out_weight, "seq", axis=1, tiled=True),
        preferred_element_type=jnp.float32,
    )
    mixed = lax.psum_scatter(terms, "tensor", scatter_dimension=1, tiled=True)
    return mixed


def solution(mesh):
    return jax.shard_map(
        per_device,
        mesh=mesh,
        in_specs=(
            P("seq", "tensor"),
            P("seq", "tensor"),
            P("seq", "tensor"),
            P("seq", "tensor"),
            P("seq", "tensor"),
            P("tensor", None, None),
            P("tensor"),
            P("tensor", "seq"),
        ),
        out_specs=P("seq", "tensor"),
        check_vma=False,
    )
```

```python
import jax
import jax.numpy as jnp
from jax import lax
from jax.sharding import PartitionSpec as P

HIGH = lax.Precision.HIGHEST


def entering(array, axis, combine, identity):
    length, mine = (lax.axis_size(axis), lax.axis_index(axis))
    everything = jax.tree.map(lambda part: lax.all_gather(part, axis), array)
    start = jax.tree.map(
        lambda part, zero: jnp.broadcast_to(jnp.asarray(zero, part.dtype), part.shape),
        array,
        identity,
    )

    def hop(k, before):
        reached = k < mine
        new = combine(before, jax.tree.map(lambda part: part[k], everything))
        return jax.tree.map(lambda a, b: jnp.where(reached, a, b), new, before)

    return lax.fori_loop(0, length, hop, start)


def block_step(state, pieces):
    queries_b, keys_b, values_b, decay_b = pieces
    cumulative_memory = jnp.cumsum(decay_b, axis=0)
    total = cumulative_memory[-1]
    carried = jnp.exp(cumulative_memory)[:, :, None] * jnp.einsum(
        "thd,hde->the", queries_b.astype(jnp.float32), state, precision=HIGH
    )
    scores = jnp.einsum("thd,shd->hts", queries_b, keys_b, preferred_element_type=jnp.float32)
    length = cumulative_memory.shape[0]
    lower = jnp.tril(jnp.ones((length, length), dtype=bool))[None]
    spread = cumulative_memory.T[:, :, None] - cumulative_memory.T[:, None, :]
    weights = jnp.where(lower, jnp.exp(jnp.where(lower, spread, 0.0)), 0.0)
    mixes = (scores * weights).astype(jnp.bfloat16)
    local = jnp.einsum("hts,she->the", mixes, values_b, preferred_element_type=jnp.float32)
    scaled = keys_b.astype(jnp.float32) * jnp.exp(total[None, :] - cumulative_memory)[:, :, None]
    new_state = jnp.exp(total)[:, None, None] * state + jnp.einsum(
        "shd,she->hde", scaled, values_b.astype(jnp.float32), precision=HIGH
    )
    return (new_state, carried + local)


def normalize(attended, norm_gain, gate_logits):
    mean_square = jnp.mean(attended * attended, axis=-1, keepdims=True)
    normalized_output = attended * lax.rsqrt(mean_square + 1e-05)
    flat = normalized_output.reshape(attended.shape[0], -1)
    gated = flat * norm_gain[None, :] * jax.nn.sigmoid(gate_logits.astype(jnp.float32))
    return gated.astype(jnp.bfloat16)


def chain_link(earlier, later):
    return (earlier[0] * later[0], later[0][:, None, None] * earlier[1] + later[1])


def pack(rates, state):
    heads = state.shape[0]
    flat = state.reshape(heads, -1)
    lanes = jnp.broadcast_to(rates[:, None], (heads, 128))
    return jnp.concatenate([flat, lanes], axis=1)


def link_packed(earlier, later):
    width = later.shape[1] - 128
    later_rate = later[:, width:width + 1]
    state = later_rate * earlier[:, :width] + later[:, :width]
    rate = earlier[:, width:] * later[:, width:]
    return jnp.concatenate([state, rate], axis=1)


def carried_in(rates, state, initial_state):
    length, mine = (lax.axis_size("seq"), lax.axis_index("seq"))
    own = pack(rates, state)
    shifted = lax.ppermute(own, "seq", [(i, i + 1) for i in range(length - 1)])
    first = pack(jnp.ones_like(rates), initial_state)
    current = jnp.where(mine == 0, first, shifted)
    step = 1
    while step < length:
        earlier = lax.ppermute(current, "seq", [(i, i + step) for i in range(length - step)])
        current = jnp.where(mine >= step, link_packed(earlier, current), current)
        step *= 2
    width = current.shape[1] - 128
    return current[:, :width].reshape(state.shape)

def per_device(
    queries, key_vectors, value_rows, gate_logits, log_decay, initial_state, norm_gain, out_weight
):
    rows_here = queries.shape[0]
    head_count = log_decay.shape[1]
    head_dim = initial_state.shape[1]
    block_len = min(512, rows_here)
    block_count = rows_here // block_len

    def shaped(array):
        return array.reshape(block_count, block_len, head_count, head_dim)

    zero_state = jnp.zeros((head_count, head_dim, head_dim), jnp.float32)
    decay_blocks = log_decay.reshape(block_count, block_len, head_count)
    device_state, outputs = lax.scan(
        block_step,
        zero_state,
        (shaped(queries), shaped(key_vectors), shaped(value_rows), decay_blocks),
    )
    local_out = outputs.reshape(rows_here, head_count, head_dim)
    through = jnp.cumsum(log_decay, axis=0)
    shard_fading_rates = jnp.exp(through[-1])
    incoming = carried_in(shard_fading_rates, device_state, initial_state)
    query_float = queries.reshape(rows_here, head_count, head_dim).astype(jnp.float32)
    inherited = jnp.exp(through)[:, :, None] * jnp.einsum(
        "thd,hde->the", query_float, incoming, precision=HIGH
    )
    attended = local_out + inherited
    hidden = normalize(attended, norm_gain, gate_logits)
    seq_len, tensor_len = (lax.axis_size("seq"), lax.axis_size("tensor"))
    col_blocks = seq_len // tensor_len
    route = []
    for s in range(seq_len):
        for t in range(tensor_len):
            source = (col_blocks * t + s // tensor_len) * tensor_len + s % tensor_len
            route.append((source, s * tensor_len + t))
    placed = lax.ppermute(out_weight, ("seq", "tensor"), route)
    columns = lax.all_gather(placed, "seq", axis=0, tiled=True)
    columns = columns.reshape(col_blocks, -1, columns.shape[1])
    full_hidden = lax.all_gather(hidden, "tensor", axis=1, tiled=True)
    mixed = jnp.einsum("tk,rkc->trc", full_hidden, columns, preferred_element_type=jnp.float32)
    mixed = mixed.reshape(rows_here, -1)
    return mixed


def solution(mesh):
    return jax.shard_map(
        per_device,
        mesh=mesh,
        in_specs=(
            P("seq", "tensor"),
            P("seq", "tensor"),
            P("seq", "tensor"),
            P("seq", "tensor"),
            P("seq", "tensor"),
            P("tensor", None, None),
            P("tensor"),
            P("tensor", "seq"),
        ),
        out_specs=P("seq", "tensor"),
        check_vma=False,
    )
```

```python
import jax
import jax.numpy as jnp
from jax import lax
from jax.sharding import Mesh, PartitionSpec as P

HIGH = lax.Precision.HIGHEST


def entering(array, axis, combine, identity):
    length, mine = (lax.axis_size(axis), lax.axis_index(axis))
    everything = jax.tree.map(lambda part: lax.all_gather(part, axis), array)
    start = jax.tree.map(
        lambda part, zero: jnp.broadcast_to(jnp.asarray(zero, part.dtype), part.shape),
        array,
        identity,
    )

    def hop(k, before):
        reached = k < mine
        new = combine(before, jax.tree.map(lambda part: part[k], everything))
        return jax.tree.map(lambda a, b: jnp.where(reached, a, b), new, before)

    return lax.fori_loop(0, length, hop, start)


def block_step(state, pieces):
    queries_b, keys_b, values_b, decay_b = pieces
    cumulative_memory = jnp.cumsum(decay_b, axis=0)
    total = cumulative_memory[-1]
    carried = jnp.exp(cumulative_memory)[:, :, None] * jnp.einsum(
        "thd,hde->the", queries_b.astype(jnp.float32), state, precision=HIGH
    )
    scores = jnp.einsum("thd,shd->hts", queries_b, keys_b, preferred_element_type=jnp.float32)
    length = cumulative_memory.shape[0]
    lower = jnp.tril(jnp.ones((length, length), dtype=bool))[None]
    spread = cumulative_memory.T[:, :, None] - cumulative_memory.T[:, None, :]
    weights = jnp.where(lower, jnp.exp(jnp.where(lower, spread, 0.0)), 0.0)
    mixes = (scores * weights).astype(jnp.bfloat16)
    local = jnp.einsum("hts,she->the", mixes, values_b, preferred_element_type=jnp.float32)
    scaled = keys_b.astype(jnp.float32) * jnp.exp(total[None, :] - cumulative_memory)[:, :, None]
    new_state = jnp.exp(total)[:, None, None] * state + jnp.einsum(
        "shd,she->hde", scaled, values_b.astype(jnp.float32), precision=HIGH
    )
    return (new_state, carried + local)


def normalize(attended, norm_gain, gate_logits):
    mean_square = jnp.mean(attended * attended, axis=-1, keepdims=True)
    normalized_output = attended * lax.rsqrt(mean_square + 1e-05)
    flat = normalized_output.reshape(attended.shape[0], -1)
    gated = flat * norm_gain[None, :] * jax.nn.sigmoid(gate_logits.astype(jnp.float32))
    return gated.astype(jnp.bfloat16)


def chain_link(earlier, later):
    return (earlier[0] * later[0], later[0][:, None, None] * earlier[1] + later[1])


def pack(rates, state):
    heads = state.shape[0]
    flat = state.reshape(heads, -1)
    lanes = jnp.broadcast_to(rates[:, None], (heads, 128))
    return jnp.concatenate([flat, lanes], axis=1)


def link_packed(earlier, later):
    width = later.shape[1] - 128
    later_rate = later[:, width:width + 1]
    state = later_rate * earlier[:, :width] + later[:, :width]
    rate = earlier[:, width:] * later[:, width:]
    return jnp.concatenate([state, rate], axis=1)


def swap_cores(array):
    return lax.ppermute(array, "core", [(0, 1), (1, 0)])


def carried_in(rates, state, initial_state):
    chips, chip = (lax.axis_size("chip"), lax.axis_index("chip"))
    core = lax.axis_index("core")
    half = state.shape[0] // 2
    own = pack(rates, state)
    own_mine = lax.dynamic_slice_in_dim(own, core * half, half, axis=0)
    own_other = lax.dynamic_slice_in_dim(own, (1 - core) * half, half, axis=0)
    partner_mine = swap_cores(own_other)
    first_core = jnp.where(core == 0, own_mine, partner_mine)
    second_core = jnp.where(core == 0, partner_mine, own_mine)
    chip_element = link_packed(first_core, second_core)
    shifted = lax.ppermute(chip_element, "chip", [(i, i + 1) for i in range(chips - 1)])
    start_state = lax.dynamic_slice_in_dim(initial_state, core * half, half, axis=0)
    first = pack(jnp.ones((half,), rates.dtype), start_state)
    current = jnp.where(chip == 0, first, shifted)
    step = 1
    while step < chips:
        earlier = lax.ppermute(current, "chip", [(i, i + step) for i in range(chips - step)])
        current = jnp.where(chip >= step, link_packed(earlier, current), current)
        step *= 2
    for_second = link_packed(current, first_core)
    keep = jnp.where(core == 0, current, for_second)
    other = swap_cores(jnp.where(core == 0, for_second, current))
    whole = jnp.where(core == 0, jnp.concatenate([keep, other]), jnp.concatenate([other, keep]))
    width = whole.shape[1] - 128
    return whole[:, :width].reshape(state.shape)


def per_device(
    queries, key_vectors, value_rows, gate_logits, log_decay, initial_state, norm_gain, out_weight
):
    rows_here = queries.shape[0]
    head_count = log_decay.shape[1]
    head_dim = initial_state.shape[1]
    block_len = min(512, rows_here)
    block_count = rows_here // block_len

    def shaped(array):
        return array.reshape(block_count, block_len, head_count, head_dim)

    zero_state = jnp.zeros((head_count, head_dim, head_dim), jnp.float32)
    decay_blocks = log_decay.reshape(block_count, block_len, head_count)
    device_state, outputs = lax.scan(
        block_step,
        zero_state,
        (shaped(queries), shaped(key_vectors), shaped(value_rows), decay_blocks),
    )
    local_out = outputs.reshape(rows_here, head_count, head_dim)
    through = jnp.cumsum(log_decay, axis=0)
    shard_fading_rates = jnp.exp(through[-1])
    incoming = carried_in(shard_fading_rates, device_state, initial_state)
    query_float = queries.reshape(rows_here, head_count, head_dim).astype(jnp.float32)
    inherited = jnp.exp(through)[:, :, None] * jnp.einsum(
        "thd,hde->the", query_float, incoming, precision=HIGH
    )
    attended = local_out + inherited
    hidden = normalize(attended, norm_gain, gate_logits)
    chips, cores, groups = (lax.axis_size("chip"), lax.axis_size("core"), lax.axis_size("tensor"))
    core = lax.axis_index("core")
    seq_len = chips * cores
    col_blocks = seq_len // groups
    quarter = chips // col_blocks
    route = []
    for q in range(chips):
        for c in range(cores):
            for t in range(groups):
                source = (col_blocks * t + q // quarter) * groups + (groups // cores) * c + q % quarter
                route.append((source, (q * cores + c) * groups + t))
    placed = lax.ppermute(out_weight, ("chip", "core", "tensor"), route)
    columns = lax.all_gather(placed, "chip", axis=0, tiled=False)
    columns = columns.reshape(col_blocks, -1, columns.shape[-1])
    width = columns.shape[1]
    full_hidden = lax.all_gather(hidden, "tensor", axis=1, tiled=True)
    mine = lax.dynamic_slice_in_dim(full_hidden, core * width, width, axis=1)
    theirs = swap_cores(lax.dynamic_slice_in_dim(full_hidden, (1 - core) * width, width, axis=1))
    own_part = jnp.einsum("tk,rkc->trc", mine, columns, preferred_element_type=jnp.float32)
    their_part = jnp.einsum("tk,rkc->trc", theirs, columns, preferred_element_type=jnp.float32)
    mixed = (own_part + swap_cores(their_part)).reshape(rows_here, -1)
    return mixed


def solution(mesh):
    seq_len, groups = mesh.devices.shape
    split = Mesh(mesh.devices.reshape(seq_len // 2, 2, groups), ("chip", "core", "tensor"))
    tokens = ("chip", "core")
    return jax.shard_map(
        per_device,
        mesh=split,
        in_specs=(
            P(tokens, "tensor"),
            P(tokens, "tensor"),
            P(tokens, "tensor"),
            P(tokens, "tensor"),
            P(tokens, "tensor"),
            P("tensor", None, None),
            P("tensor"),
            P("tensor", tokens),
        ),
        out_specs=P(tokens, "tensor"),
        check_vma=False,
    )
```

```python
import jax
import jax.numpy as jnp
from jax import lax
from jax.sharding import Mesh, PartitionSpec as P

HIGH = lax.Precision.HIGHEST


def entering(array, axis, combine, identity):
    length, mine = (lax.axis_size(axis), lax.axis_index(axis))
    everything = jax.tree.map(lambda part: lax.all_gather(part, axis), array)
    start = jax.tree.map(
        lambda part, zero: jnp.broadcast_to(jnp.asarray(zero, part.dtype), part.shape),
        array,
        identity,
    )

    def hop(k, before):
        reached = k < mine
        new = combine(before, jax.tree.map(lambda part: part[k], everything))
        return jax.tree.map(lambda a, b: jnp.where(reached, a, b), new, before)

    return lax.fori_loop(0, length, hop, start)


def block_step(state, pieces):
    queries_b, keys_b, values_b, decay_b = pieces
    cumulative_memory = jnp.cumsum(decay_b, axis=0)
    total = cumulative_memory[-1]
    carried = jnp.exp(cumulative_memory)[:, :, None] * jnp.einsum(
        "thd,hde->the", queries_b.astype(jnp.float32), state, precision=HIGH
    )
    scores = jnp.einsum("thd,shd->hts", queries_b, keys_b, preferred_element_type=jnp.float32)
    length = cumulative_memory.shape[0]
    lower = jnp.tril(jnp.ones((length, length), dtype=bool))[None]
    spread = cumulative_memory.T[:, :, None] - cumulative_memory.T[:, None, :]
    weights = jnp.where(lower, jnp.exp(jnp.where(lower, spread, 0.0)), 0.0)
    mixes = (scores * weights).astype(jnp.bfloat16)
    local = jnp.einsum("hts,she->the", mixes, values_b, preferred_element_type=jnp.float32)
    scaled = keys_b.astype(jnp.float32) * jnp.exp(total[None, :] - cumulative_memory)[:, :, None]
    new_state = jnp.exp(total)[:, None, None] * state + jnp.einsum(
        "shd,she->hde", scaled, values_b.astype(jnp.float32), precision=HIGH
    )
    return (new_state, carried + local)


def normalize(attended, norm_gain, gate_logits):
    mean_square = jnp.mean(attended * attended, axis=-1, keepdims=True)
    normalized_output = attended * lax.rsqrt(mean_square + 1e-05)
    flat = normalized_output.reshape(attended.shape[0], -1)
    gated = flat * norm_gain[None, :] * jax.nn.sigmoid(gate_logits.astype(jnp.float32))
    return gated.astype(jnp.bfloat16)


def chain_link(earlier, later):
    return (earlier[0] * later[0], later[0][:, None, None] * earlier[1] + later[1])


def pack(rates, state):
    heads = state.shape[0]
    flat = state.reshape(heads, -1)
    lanes = jnp.broadcast_to(rates[:, None], (heads, 128))
    return jnp.concatenate([flat, lanes], axis=1)


def link_packed(earlier, later):
    width = later.shape[1] - 128
    later_rate = later[:, width:width + 1]
    state = later_rate * earlier[:, :width] + later[:, :width]
    rate = earlier[:, width:] * later[:, width:]
    return jnp.concatenate([state, rate], axis=1)


def swap_cores(array):
    return lax.ppermute(array, "core", [(0, 1), (1, 0)])


def carried_in(rates, state, initial_state):
    chips, chip = (lax.axis_size("chip"), lax.axis_index("chip"))
    core = lax.axis_index("core")
    half = state.shape[0] // 2
    own = pack(rates, state)
    own_mine = lax.dynamic_slice_in_dim(own, core * half, half, axis=0)
    own_other = lax.dynamic_slice_in_dim(own, (1 - core) * half, half, axis=0)
    partner_mine = swap_cores(own_other)
    first_core = jnp.where(core == 0, own_mine, partner_mine)
    second_core = jnp.where(core == 0, partner_mine, own_mine)
    chip_element = link_packed(first_core, second_core)
    shifted = lax.ppermute(chip_element, "chip", [(i, i + 1) for i in range(chips - 1)])
    start_state = lax.dynamic_slice_in_dim(initial_state, core * half, half, axis=0)
    first = pack(jnp.ones((half,), rates.dtype), start_state)
    current = jnp.where(chip == 0, first, shifted)
    step = 1
    while step < chips:
        earlier = lax.ppermute(current, "chip", [(i, i + step) for i in range(chips - step)])
        current = jnp.where(chip >= step, link_packed(earlier, current), current)
        step *= 2
    for_second = link_packed(current, first_core)
    keep = jnp.where(core == 0, current, for_second)
    other = swap_cores(jnp.where(core == 0, for_second, current))
    whole = jnp.where(core == 0, jnp.concatenate([keep, other]), jnp.concatenate([other, keep]))
    width = whole.shape[1] - 128
    return whole[:, :width].reshape(state.shape)


def place_columns(out_weight):
    chips, cores, groups = (lax.axis_size("chip"), lax.axis_size("core"), lax.axis_size("tensor"))
    col_blocks = chips * cores // groups
    quarter = chips // col_blocks
    route = []
    for q in range(chips):
        for c in range(cores):
            for t in range(groups):
                source = (col_blocks * t + q // quarter) * groups + (groups // cores) * c + q % quarter
                route.append((source, (q * cores + c) * groups + t))
    return lax.ppermute(out_weight, ("chip", "core", "tensor"), route)


def gather_groups(block):
    groups, mine = (lax.axis_size("tensor"), lax.axis_index("tensor"))
    up = [(i, (i + 1) % groups) for i in range(groups)]
    down = [(i, (i - 1) % groups) for i in range(groups)]
    from_below, from_above = [], []
    below, above = block, block
    for _ in range(groups // 2):
        below = lax.ppermute(below, "tensor", up)
        from_below.append(below)
        if len(from_above) < (groups - 1) // 2:
            above = lax.ppermute(above, "tensor", down)
            from_above.append(above)
    relative = jnp.concatenate([block] + from_above + from_below[::-1], axis=1)
    return jnp.roll(relative, mine * block.shape[1], axis=1)


def per_device(
    queries, key_vectors, value_rows, gate_logits, log_decay, initial_state, norm_gain, out_weight
):
    rows_here = queries.shape[0]
    head_count = log_decay.shape[1]
    head_dim = initial_state.shape[1]
    block_len = min(512, rows_here)
    block_count = rows_here // block_len

    def shaped(array):
        return array.reshape(block_count, block_len, head_count, head_dim)

    placed = place_columns(out_weight)
    placed, queries = lax.optimization_barrier((placed, queries))
    zero_state = jnp.zeros((head_count, head_dim, head_dim), jnp.float32)
    decay_blocks = log_decay.reshape(block_count, block_len, head_count)
    device_state, outputs = lax.scan(
        block_step,
        zero_state,
        (shaped(queries), shaped(key_vectors), shaped(value_rows), decay_blocks),
    )
    local_out = outputs.reshape(rows_here, head_count, head_dim)
    through = jnp.cumsum(log_decay, axis=0)
    shard_fading_rates = jnp.exp(through[-1])
    incoming = carried_in(shard_fading_rates, device_state, initial_state)
    query_float = queries.reshape(rows_here, head_count, head_dim).astype(jnp.float32)
    inherited = jnp.exp(through)[:, :, None] * jnp.einsum(
        "thd,hde->the", query_float, incoming, precision=HIGH
    )
    attended = local_out + inherited
    hidden = normalize(attended, norm_gain, gate_logits)
    chips, cores, groups = (lax.axis_size("chip"), lax.axis_size("core"), lax.axis_size("tensor"))
    core = lax.axis_index("core")
    seq_len = chips * cores
    col_blocks = seq_len // groups
    quarter = chips // col_blocks
    columns = lax.all_gather(placed, "chip", axis=0, tiled=False)
    columns = columns.reshape(col_blocks, -1, columns.shape[-1])
    width = columns.shape[1]
    full_hidden = gather_groups(hidden)
    mine = lax.dynamic_slice_in_dim(full_hidden, core * width, width, axis=1)
    theirs = swap_cores(lax.dynamic_slice_in_dim(full_hidden, (1 - core) * width, width, axis=1))
    own_part = jnp.einsum("tk,rkc->trc", mine, columns, preferred_element_type=jnp.float32)
    their_part = jnp.einsum("tk,rkc->trc", theirs, columns, preferred_element_type=jnp.float32)
    mixed = (own_part + swap_cores(their_part)).reshape(rows_here, -1)
    return mixed


def solution(mesh):
    seq_len, groups = mesh.devices.shape
    split = Mesh(mesh.devices.reshape(seq_len // 2, 2, groups), ("chip", "core", "tensor"))
    tokens = ("chip", "core")
    return jax.shard_map(
        per_device,
        mesh=split,
        in_specs=(
            P(tokens, "tensor"),
            P(tokens, "tensor"),
            P(tokens, "tensor"),
            P(tokens, "tensor"),
            P(tokens, "tensor"),
            P("tensor", None, None),
            P("tensor"),
            P("tensor", tokens),
        ),
        out_specs=P(tokens, "tensor"),
        check_vma=False,
    )
```

```python
import jax
import jax.numpy as jnp
from jax import lax
from jax.sharding import Mesh, PartitionSpec as P

HIGH = lax.Precision.HIGHEST


def entering(array, axis, combine, identity):
    length, mine = (lax.axis_size(axis), lax.axis_index(axis))
    everything = jax.tree.map(lambda part: lax.all_gather(part, axis), array)
    start = jax.tree.map(
        lambda part, zero: jnp.broadcast_to(jnp.asarray(zero, part.dtype), part.shape),
        array,
        identity,
    )

    def hop(k, before):
        reached = k < mine
        new = combine(before, jax.tree.map(lambda part: part[k], everything))
        return jax.tree.map(lambda a, b: jnp.where(reached, a, b), new, before)

    return lax.fori_loop(0, length, hop, start)


def block_step(state, pieces):
    queries_b, keys_b, values_b, decay_b = pieces
    cumulative_memory = jnp.cumsum(decay_b, axis=0)
    total = cumulative_memory[-1]
    carried = jnp.exp(cumulative_memory)[:, :, None] * jnp.einsum(
        "thd,hde->the", queries_b.astype(jnp.float32), state, precision=HIGH
    )
    scores = jnp.einsum("thd,shd->hts", queries_b, keys_b, preferred_element_type=jnp.float32)
    length = cumulative_memory.shape[0]
    lower = jnp.tril(jnp.ones((length, length), dtype=bool))[None]
    spread = cumulative_memory.T[:, :, None] - cumulative_memory.T[:, None, :]
    weights = jnp.where(lower, jnp.exp(jnp.where(lower, spread, 0.0)), 0.0)
    mixes = (scores * weights).astype(jnp.bfloat16)
    local = jnp.einsum("hts,she->the", mixes, values_b, preferred_element_type=jnp.float32)
    scaled = keys_b.astype(jnp.float32) * jnp.exp(total[None, :] - cumulative_memory)[:, :, None]
    new_state = jnp.exp(total)[:, None, None] * state + jnp.einsum(
        "shd,she->hde", scaled, values_b.astype(jnp.float32), precision=HIGH
    )
    return (new_state, carried + local)


def normalize(attended, norm_gain, gate_logits):
    mean_square = jnp.mean(attended * attended, axis=-1, keepdims=True)
    normalized_output = attended * lax.rsqrt(mean_square + 1e-05)
    flat = normalized_output.reshape(attended.shape[0], -1)
    gated = flat * norm_gain[None, :] * jax.nn.sigmoid(gate_logits.astype(jnp.float32))
    return gated.astype(jnp.bfloat16)


def chain_link(earlier, later):
    return (earlier[0] * later[0], later[0][:, None, None] * earlier[1] + later[1])


def pack(rates, state):
    heads = state.shape[0]
    flat = state.reshape(heads, -1)
    lanes = jnp.broadcast_to(rates[:, None], (heads, 128))
    return jnp.concatenate([flat, lanes], axis=1)


def link_packed(earlier, later):
    width = later.shape[1] - 128
    later_rate = later[:, width:width + 1]
    state = later_rate * earlier[:, :width] + later[:, :width]
    rate = earlier[:, width:] * later[:, width:]
    return jnp.concatenate([state, rate], axis=1)


def swap_cores(array):
    return lax.ppermute(array, "core", [(0, 1), (1, 0)])


def carried_in(rates, state, initial_state):
    chips, chip = (lax.axis_size("chip"), lax.axis_index("chip"))
    core = lax.axis_index("core")
    half = state.shape[0] // 2
    own = pack(rates, state)
    own_mine = lax.dynamic_slice_in_dim(own, core * half, half, axis=0)
    own_other = lax.dynamic_slice_in_dim(own, (1 - core) * half, half, axis=0)
    partner_mine = swap_cores(own_other)
    first_core = jnp.where(core == 0, own_mine, partner_mine)
    second_core = jnp.where(core == 0, partner_mine, own_mine)
    chip_element = link_packed(first_core, second_core)
    shifted = lax.ppermute(chip_element, "chip", [(i, i + 1) for i in range(chips - 1)])
    start_state = lax.dynamic_slice_in_dim(initial_state, core * half, half, axis=0)
    first = pack(jnp.ones((half,), rates.dtype), start_state)
    current = jnp.where(chip == 0, first, shifted)
    step = 1
    while step < chips:
        earlier = lax.ppermute(current, "chip", [(i, i + step) for i in range(chips - step)])
        current = jnp.where(chip >= step, link_packed(earlier, current), current)
        step *= 2
    for_second = link_packed(current, first_core)
    keep = jnp.where(core == 0, current, for_second)
    other = swap_cores(jnp.where(core == 0, for_second, current))
    whole = jnp.where(core == 0, jnp.concatenate([keep, other]), jnp.concatenate([other, keep]))
    width = whole.shape[1] - 128
    return whole[:, :width].reshape(state.shape)


def per_device(
    queries, key_vectors, value_rows, gate_logits, log_decay, initial_state, norm_gain, out_weight
):
    rows_here = queries.shape[0]
    head_count = log_decay.shape[1]
    head_dim = initial_state.shape[1]
    block_len = min(512, rows_here)
    block_count = rows_here // block_len

    def shaped(array):
        return array.reshape(block_count, block_len, head_count, head_dim)

    zero_state = jnp.zeros((head_count, head_dim, head_dim), jnp.float32)
    decay_blocks = log_decay.reshape(block_count, block_len, head_count)
    device_state, outputs = lax.scan(
        block_step,
        zero_state,
        (shaped(queries), shaped(key_vectors), shaped(value_rows), decay_blocks),
    )
    local_out = outputs.reshape(rows_here, head_count, head_dim)
    through = jnp.cumsum(log_decay, axis=0)
    shard_fading_rates = jnp.exp(through[-1])
    incoming = carried_in(shard_fading_rates, device_state, initial_state)
    query_float = queries.reshape(rows_here, head_count, head_dim).astype(jnp.float32)
    inherited = jnp.exp(through)[:, :, None] * jnp.einsum(
        "thd,hde->the", query_float, incoming, precision=HIGH
    )
    attended = local_out + inherited
    hidden = normalize(attended, norm_gain, gate_logits)
    terms = jnp.dot(
        hidden,
        lax.all_gather(out_weight, ("chip", "core"), axis=1, tiled=True),
        preferred_element_type=jnp.float32,
    )
    mixed = lax.psum_scatter(terms, "tensor", scatter_dimension=1, tiled=True)
    return mixed


def solution(mesh):
    seq_len, groups = mesh.devices.shape
    split = Mesh(mesh.devices.reshape(seq_len // 2, 2, groups), ("chip", "core", "tensor"))
    tokens = ("chip", "core")
    return jax.shard_map(
        per_device,
        mesh=split,
        in_specs=(
            P(tokens, "tensor"),
            P(tokens, "tensor"),
            P(tokens, "tensor"),
            P(tokens, "tensor"),
            P(tokens, "tensor"),
            P("tensor", None, None),
            P("tensor"),
            P("tensor", tokens),
        ),
        out_specs=P(tokens, "tensor"),
        check_vma=False,
    )
```

```python
import jax
import jax.numpy as jnp
from jax import lax
from jax.sharding import Mesh, PartitionSpec as P

HIGH = lax.Precision.HIGHEST


def entering(array, axis, combine, identity):
    length, mine = (lax.axis_size(axis), lax.axis_index(axis))
    everything = jax.tree.map(lambda part: lax.all_gather(part, axis), array)
    start = jax.tree.map(
        lambda part, zero: jnp.broadcast_to(jnp.asarray(zero, part.dtype), part.shape),
        array,
        identity,
    )

    def hop(k, before):
        reached = k < mine
        new = combine(before, jax.tree.map(lambda part: part[k], everything))
        return jax.tree.map(lambda a, b: jnp.where(reached, a, b), new, before)

    return lax.fori_loop(0, length, hop, start)


def block_step(state, pieces):
    queries_b, keys_b, values_b, decay_b = pieces
    cumulative_memory = jnp.cumsum(decay_b, axis=0)
    total = cumulative_memory[-1]
    carried = jnp.exp(cumulative_memory)[:, :, None] * jnp.einsum(
        "thd,hde->the", queries_b.astype(jnp.float32), state, precision=HIGH
    )
    scores = jnp.einsum("thd,shd->hts", queries_b, keys_b, preferred_element_type=jnp.float32)
    length = cumulative_memory.shape[0]
    lower = jnp.tril(jnp.ones((length, length), dtype=bool))[None]
    spread = cumulative_memory.T[:, :, None] - cumulative_memory.T[:, None, :]
    weights = jnp.where(lower, jnp.exp(jnp.where(lower, spread, 0.0)), 0.0)
    mixes = (scores * weights).astype(jnp.bfloat16)
    local = jnp.einsum("hts,she->the", mixes, values_b, preferred_element_type=jnp.float32)
    scaled = keys_b.astype(jnp.float32) * jnp.exp(total[None, :] - cumulative_memory)[:, :, None]
    new_state = jnp.exp(total)[:, None, None] * state + jnp.einsum(
        "shd,she->hde", scaled, values_b.astype(jnp.float32), precision=HIGH
    )
    return (new_state, carried + local)


def normalize(attended, norm_gain, gate_logits):
    mean_square = jnp.mean(attended * attended, axis=-1, keepdims=True)
    normalized_output = attended * lax.rsqrt(mean_square + 1e-05)
    flat = normalized_output.reshape(attended.shape[0], -1)
    gated = flat * norm_gain[None, :] * jax.nn.sigmoid(gate_logits.astype(jnp.float32))
    return gated.astype(jnp.bfloat16)


def chain_link(earlier, later):
    return (earlier[0] * later[0], later[0][:, None, None] * earlier[1] + later[1])


def pack(rates, state):
    heads = state.shape[0]
    flat = state.reshape(heads, -1)
    lanes = jnp.broadcast_to(rates[:, None], (heads, 128))
    return jnp.concatenate([flat, lanes], axis=1)


def link_packed(earlier, later):
    width = later.shape[1] - 128
    later_rate = later[:, width:width + 1]
    state = later_rate * earlier[:, :width] + later[:, :width]
    rate = earlier[:, width:] * later[:, width:]
    return jnp.concatenate([state, rate], axis=1)


def swap_cores(array):
    return lax.ppermute(array, "core", [(0, 1), (1, 0)])


def carried_in(rates, state, initial_state):
    chips, chip = (lax.axis_size("chip"), lax.axis_index("chip"))
    core = lax.axis_index("core")
    half = state.shape[0] // 2
    own = pack(rates, state)
    own_mine = lax.dynamic_slice_in_dim(own, core * half, half, axis=0)
    own_other = lax.dynamic_slice_in_dim(own, (1 - core) * half, half, axis=0)
    partner_mine = swap_cores(own_other)
    first_core = jnp.where(core == 0, own_mine, partner_mine)
    second_core = jnp.where(core == 0, partner_mine, own_mine)
    chip_element = link_packed(first_core, second_core)
    shifted = lax.ppermute(chip_element, "chip", [(i, i + 1) for i in range(chips - 1)])
    start_state = lax.dynamic_slice_in_dim(initial_state, core * half, half, axis=0)
    first = pack(jnp.ones((half,), rates.dtype), start_state)
    current = jnp.where(chip == 0, first, shifted)
    step = 1
    while step < chips:
        earlier = lax.ppermute(current, "chip", [(i, i + step) for i in range(chips - step)])
        current = jnp.where(chip >= step, link_packed(earlier, current), current)
        step *= 2
    for_second = link_packed(current, first_core)
    keep = jnp.where(core == 0, current, for_second)
    other = swap_cores(jnp.where(core == 0, for_second, current))
    whole = jnp.where(core == 0, jnp.concatenate([keep, other]), jnp.concatenate([other, keep]))
    width = whole.shape[1] - 128
    return whole[:, :width].reshape(state.shape)


def place_columns(out_weight):
    chips, cores, groups = (lax.axis_size("chip"), lax.axis_size("core"), lax.axis_size("tensor"))
    seq_len = chips * cores
    col_blocks = seq_len // groups
    route = []
    for s in range(seq_len):
        for t in range(groups):
            source = (col_blocks * t + s % col_blocks) * groups + (t + s // col_blocks) % groups
            route.append((source, s * groups + t))
    return lax.ppermute(out_weight, ("chip", "core", "tensor"), route)


def gather_groups(block):
    groups = lax.axis_size("tensor")
    up = [(i, (i + 1) % groups) for i in range(groups)]
    down = [(i, (i - 1) % groups) for i in range(groups)]
    from_below, from_above = [], []
    below, above = block, block
    for _ in range(groups // 2):
        below = lax.ppermute(below, "tensor", up)
        from_below.append(below)
        if len(from_above) < (groups - 1) // 2:
            above = lax.ppermute(above, "tensor", down)
            from_above.append(above)
    return jnp.concatenate([block] + from_above + from_below[::-1], axis=1)


def per_device(
    queries, key_vectors, value_rows, gate_logits, log_decay, initial_state, norm_gain, out_weight
):
    rows_here = queries.shape[0]
    head_count = log_decay.shape[1]
    head_dim = initial_state.shape[1]
    block_len = min(512, rows_here)
    block_count = rows_here // block_len

    def shaped(array):
        return array.reshape(block_count, block_len, head_count, head_dim)

    placed = place_columns(out_weight)
    zero_state = jnp.zeros((head_count, head_dim, head_dim), jnp.float32)
    decay_blocks = log_decay.reshape(block_count, block_len, head_count)
    device_state, outputs = lax.scan(
        block_step,
        zero_state,
        (shaped(queries), shaped(key_vectors), shaped(value_rows), decay_blocks),
    )
    local_out = outputs.reshape(rows_here, head_count, head_dim)
    through = jnp.cumsum(log_decay, axis=0)
    shard_fading_rates = jnp.exp(through[-1])
    incoming = carried_in(shard_fading_rates, device_state, initial_state)
    query_float = queries.reshape(rows_here, head_count, head_dim).astype(jnp.float32)
    inherited = jnp.exp(through)[:, :, None] * jnp.einsum(
        "thd,hde->the", query_float, incoming, precision=HIGH
    )
    attended = local_out + inherited
    hidden = normalize(attended, norm_gain, gate_logits)
    full_hidden = gather_groups(hidden)
    groups = lax.axis_size("tensor")
    columns = lax.all_gather(placed, ("chip", "core"), axis=1, tiled=True)
    columns = columns.reshape(columns.shape[0], groups, -1)
    stacked = full_hidden.reshape(rows_here, groups, -1)
    mixed = jnp.einsum("tjf,fjn->tn", stacked, columns, preferred_element_type=jnp.float32)
    return mixed


def solution(mesh):
    seq_len, groups = mesh.devices.shape
    split = Mesh(mesh.devices.reshape(seq_len // 2, 2, groups), ("chip", "core", "tensor"))
    tokens = ("chip", "core")
    return jax.shard_map(
        per_device,
        mesh=split,
        in_specs=(
            P(tokens, "tensor"),
            P(tokens, "tensor"),
            P(tokens, "tensor"),
            P(tokens, "tensor"),
            P(tokens, "tensor"),
            P("tensor", None, None),
            P("tensor"),
            P("tensor", tokens),
        ),
        out_specs=P(tokens, "tensor"),
        check_vma=False,
    )
```

```python
import jax
import jax.numpy as jnp
from jax import lax
from jax.sharding import Mesh, PartitionSpec as P

HIGH = lax.Precision.HIGHEST


def entering(array, axis, combine, identity):
    length, mine = (lax.axis_size(axis), lax.axis_index(axis))
    everything = jax.tree.map(lambda part: lax.all_gather(part, axis), array)
    start = jax.tree.map(
        lambda part, zero: jnp.broadcast_to(jnp.asarray(zero, part.dtype), part.shape),
        array,
        identity,
    )

    def hop(k, before):
        reached = k < mine
        new = combine(before, jax.tree.map(lambda part: part[k], everything))
        return jax.tree.map(lambda a, b: jnp.where(reached, a, b), new, before)

    return lax.fori_loop(0, length, hop, start)


def block_step(state, pieces):
    queries_b, keys_b, values_b, decay_b = pieces
    cumulative_memory = jnp.cumsum(decay_b, axis=0)
    total = cumulative_memory[-1]
    carried = jnp.exp(cumulative_memory)[:, :, None] * jnp.einsum(
        "thd,hde->the", queries_b.astype(jnp.float32), state, precision=HIGH
    )
    scores = jnp.einsum("thd,shd->hts", queries_b, keys_b, preferred_element_type=jnp.float32)
    length = cumulative_memory.shape[0]
    lower = jnp.tril(jnp.ones((length, length), dtype=bool))[None]
    spread = cumulative_memory.T[:, :, None] - cumulative_memory.T[:, None, :]
    weights = jnp.where(lower, jnp.exp(jnp.where(lower, spread, 0.0)), 0.0)
    mixes = (scores * weights).astype(jnp.bfloat16)
    local = jnp.einsum("hts,she->the", mixes, values_b, preferred_element_type=jnp.float32)
    scaled = keys_b.astype(jnp.float32) * jnp.exp(total[None, :] - cumulative_memory)[:, :, None]
    new_state = jnp.exp(total)[:, None, None] * state + jnp.einsum(
        "shd,she->hde", scaled, values_b.astype(jnp.float32), precision=HIGH
    )
    return (new_state, carried + local)


def normalize(attended, norm_gain, gate_logits):
    mean_square = jnp.mean(attended * attended, axis=-1, keepdims=True)
    normalized_output = attended * lax.rsqrt(mean_square + 1e-05)
    flat = normalized_output.reshape(attended.shape[0], -1)
    gated = flat * norm_gain[None, :] * jax.nn.sigmoid(gate_logits.astype(jnp.float32))
    return gated.astype(jnp.bfloat16)


def chain_link(earlier, later):
    return (earlier[0] * later[0], later[0][:, None, None] * earlier[1] + later[1])


def pack(rates, state):
    heads = state.shape[0]
    flat = state.reshape(heads, -1)
    lanes = jnp.broadcast_to(rates[:, None], (heads, 128))
    return jnp.concatenate([flat, lanes], axis=1)


def link_packed(earlier, later):
    width = later.shape[1] - 128
    later_rate = later[:, width:width + 1]
    state = later_rate * earlier[:, :width] + later[:, :width]
    rate = earlier[:, width:] * later[:, width:]
    return jnp.concatenate([state, rate], axis=1)


def swap_cores(array):
    return lax.ppermute(array, "core", [(0, 1), (1, 0)])


def carried_in(rates, state, initial_state):
    chips, chip = (lax.axis_size("chip"), lax.axis_index("chip"))
    core = lax.axis_index("core")
    half = state.shape[0] // 2
    own = pack(rates, state)
    own_mine = lax.dynamic_slice_in_dim(own, core * half, half, axis=0)
    own_other = lax.dynamic_slice_in_dim(own, (1 - core) * half, half, axis=0)
    partner_mine = swap_cores(own_other)
    first_core = jnp.where(core == 0, own_mine, partner_mine)
    second_core = jnp.where(core == 0, partner_mine, own_mine)
    chip_element = link_packed(first_core, second_core)
    shifted = lax.ppermute(chip_element, "chip", [(i, i + 1) for i in range(chips - 1)])
    start_state = lax.dynamic_slice_in_dim(initial_state, core * half, half, axis=0)
    first = pack(jnp.ones((half,), rates.dtype), start_state)
    current = jnp.where(chip == 0, first, shifted)
    step = 1
    while step < chips:
        earlier = lax.ppermute(current, "chip", [(i, i + step) for i in range(chips - step)])
        current = jnp.where(chip >= step, link_packed(earlier, current), current)
        step *= 2
    for_second = link_packed(current, first_core)
    keep = jnp.where(core == 0, current, for_second)
    other = swap_cores(jnp.where(core == 0, for_second, current))
    whole = jnp.where(core == 0, jnp.concatenate([keep, other]), jnp.concatenate([other, keep]))
    width = whole.shape[1] - 128
    return whole[:, :width].reshape(state.shape)


def ring_reduce_scatter(terms):
    groups, mine = (lax.axis_size("tensor"), lax.axis_index("tensor"))
    width = terms.shape[1] // groups
    half = width // 2
    up = [(i, (i + 1) % groups) for i in range(groups)]
    down = [(i, (i - 1) % groups) for i in range(groups)]

    def block(index, offset):
        return lax.dynamic_slice_in_dim(terms, (index % groups) * width + offset, half, axis=1)

    rising = block(mine - 1 + groups, 0)
    falling = block(mine + 1, half)
    for k in range(1, groups):
        rising = lax.ppermute(rising, "tensor", up) + block(mine - k - 1 + 2 * groups, 0)
        falling = lax.ppermute(falling, "tensor", down) + block(mine + k + 1, half)
    return jnp.concatenate([rising, falling], axis=1)


def per_device(
    queries, key_vectors, value_rows, gate_logits, log_decay, initial_state, norm_gain, out_weight
):
    rows_here = queries.shape[0]
    head_count = log_decay.shape[1]
    head_dim = initial_state.shape[1]
    block_len = min(512, rows_here)
    block_count = rows_here // block_len

    def shaped(array):
        return array.reshape(block_count, block_len, head_count, head_dim)

    zero_state = jnp.zeros((head_count, head_dim, head_dim), jnp.float32)
    decay_blocks = log_decay.reshape(block_count, block_len, head_count)
    device_state, outputs = lax.scan(
        block_step,
        zero_state,
        (shaped(queries), shaped(key_vectors), shaped(value_rows), decay_blocks),
    )
    local_out = outputs.reshape(rows_here, head_count, head_dim)
    through = jnp.cumsum(log_decay, axis=0)
    shard_fading_rates = jnp.exp(through[-1])
    incoming = carried_in(shard_fading_rates, device_state, initial_state)
    query_float = queries.reshape(rows_here, head_count, head_dim).astype(jnp.float32)
    inherited = jnp.exp(through)[:, :, None] * jnp.einsum(
        "thd,hde->the", query_float, incoming, precision=HIGH
    )
    attended = local_out + inherited
    hidden = normalize(attended, norm_gain, gate_logits)
    terms = jnp.dot(
        hidden,
        lax.all_gather(out_weight, ("chip", "core"), axis=1, tiled=True),
        preferred_element_type=jnp.float32,
    )
    mixed = ring_reduce_scatter(terms)
    return mixed


def solution(mesh):
    seq_len, groups = mesh.devices.shape
    split = Mesh(mesh.devices.reshape(seq_len // 2, 2, groups), ("chip", "core", "tensor"))
    tokens = ("chip", "core")
    return jax.shard_map(
        per_device,
        mesh=split,
        in_specs=(
            P(tokens, "tensor"),
            P(tokens, "tensor"),
            P(tokens, "tensor"),
            P(tokens, "tensor"),
            P(tokens, "tensor"),
            P("tensor", None, None),
            P("tensor"),
            P("tensor", tokens),
        ),
        out_specs=P(tokens, "tensor"),
        check_vma=False,
    )
```

```python
import jax
import jax.numpy as jnp
from jax import lax
from jax.sharding import Mesh, PartitionSpec as P

HIGH = lax.Precision.HIGHEST


def entering(array, axis, combine, identity):
    length, mine = (lax.axis_size(axis), lax.axis_index(axis))
    everything = jax.tree.map(lambda part: lax.all_gather(part, axis), array)
    start = jax.tree.map(
        lambda part, zero: jnp.broadcast_to(jnp.asarray(zero, part.dtype), part.shape),
        array,
        identity,
    )

    def hop(k, before):
        reached = k < mine
        new = combine(before, jax.tree.map(lambda part: part[k], everything))
        return jax.tree.map(lambda a, b: jnp.where(reached, a, b), new, before)

    return lax.fori_loop(0, length, hop, start)


def block_step(state, pieces):
    queries_b, keys_b, values_b, decay_b = pieces
    cumulative_memory = jnp.cumsum(decay_b, axis=0)
    total = cumulative_memory[-1]
    carried = jnp.exp(cumulative_memory)[:, :, None] * jnp.einsum(
        "thd,hde->the", queries_b.astype(jnp.float32), state, precision=HIGH
    )
    scores = jnp.einsum("thd,shd->hts", queries_b, keys_b, preferred_element_type=jnp.float32)
    length = cumulative_memory.shape[0]
    lower = jnp.tril(jnp.ones((length, length), dtype=bool))[None]
    spread = cumulative_memory.T[:, :, None] - cumulative_memory.T[:, None, :]
    weights = jnp.where(lower, jnp.exp(jnp.where(lower, spread, 0.0)), 0.0)
    mixes = (scores * weights).astype(jnp.bfloat16)
    local = jnp.einsum("hts,she->the", mixes, values_b, preferred_element_type=jnp.float32)
    scaled = keys_b.astype(jnp.float32) * jnp.exp(total[None, :] - cumulative_memory)[:, :, None]
    new_state = jnp.exp(total)[:, None, None] * state + jnp.einsum(
        "shd,she->hde", scaled, values_b.astype(jnp.float32), precision=HIGH
    )
    return (new_state, carried + local)


def normalize(attended, norm_gain, gate_logits):
    mean_square = jnp.mean(attended * attended, axis=-1, keepdims=True)
    normalized_output = attended * lax.rsqrt(mean_square + 1e-05)
    flat = normalized_output.reshape(attended.shape[0], -1)
    gated = flat * norm_gain[None, :] * jax.nn.sigmoid(gate_logits.astype(jnp.float32))
    return gated.astype(jnp.bfloat16)


def chain_link(earlier, later):
    return (earlier[0] * later[0], later[0][:, None, None] * earlier[1] + later[1])


def pack(rates, state):
    heads = state.shape[0]
    flat = state.reshape(heads, -1)
    lanes = jnp.broadcast_to(rates[:, None], (heads, 128))
    return jnp.concatenate([flat, lanes], axis=1)


def link_packed(earlier, later):
    width = later.shape[1] - 128
    later_rate = later[:, width:width + 1]
    state = later_rate * earlier[:, :width] + later[:, :width]
    rate = earlier[:, width:] * later[:, width:]
    return jnp.concatenate([state, rate], axis=1)


def swap_cores(array):
    return lax.ppermute(array, "core", [(0, 1), (1, 0)])


def carried_in(rates, state, initial_state):
    chips, chip = (lax.axis_size("chip"), lax.axis_index("chip"))
    core = lax.axis_index("core")
    half = state.shape[0] // 2
    own = pack(rates, state)
    own_mine = lax.dynamic_slice_in_dim(own, core * half, half, axis=0)
    own_other = lax.dynamic_slice_in_dim(own, (1 - core) * half, half, axis=0)
    partner_mine = swap_cores(own_other)
    first_core = jnp.where(core == 0, own_mine, partner_mine)
    second_core = jnp.where(core == 0, partner_mine, own_mine)
    chip_element = link_packed(first_core, second_core)
    shifted = lax.ppermute(chip_element, "chip", [(i, i + 1) for i in range(chips - 1)])
    start_state = lax.dynamic_slice_in_dim(initial_state, core * half, half, axis=0)
    first = pack(jnp.ones((half,), rates.dtype), start_state)
    current = jnp.where(chip == 0, first, shifted)
    step = 1
    while step < chips:
        earlier = lax.ppermute(current, "chip", [(i, i + step) for i in range(chips - step)])
        current = jnp.where(chip >= step, link_packed(earlier, current), current)
        step *= 2
    for_second = link_packed(current, first_core)
    keep = jnp.where(core == 0, current, for_second)
    other = swap_cores(jnp.where(core == 0, for_second, current))
    whole = jnp.where(core == 0, jnp.concatenate([keep, other]), jnp.concatenate([other, keep]))
    width = whole.shape[1] - 128
    return whole[:, :width].reshape(state.shape)


def per_device(
    queries, key_vectors, value_rows, gate_logits, log_decay, initial_state, norm_gain, out_weight
):
    rows_here = queries.shape[0]
    head_count = log_decay.shape[1]
    head_dim = initial_state.shape[1]
    block_len = min(512, rows_here)
    block_count = rows_here // block_len

    def shaped(array):
        return array.reshape(block_count, block_len, head_count, head_dim)

    zero_state = jnp.zeros((head_count, head_dim, head_dim), jnp.float32)
    decay_blocks = log_decay.reshape(block_count, block_len, head_count)
    device_state, outputs = lax.scan(
        block_step,
        zero_state,
        (shaped(queries), shaped(key_vectors), shaped(value_rows), decay_blocks),
    )
    local_out = outputs.reshape(rows_here, head_count, head_dim)
    through = jnp.cumsum(log_decay, axis=0)
    shard_fading_rates = jnp.exp(through[-1])
    incoming = carried_in(shard_fading_rates, device_state, initial_state)
    query_float = queries.reshape(rows_here, head_count, head_dim).astype(jnp.float32)
    inherited = jnp.exp(through)[:, :, None] * jnp.einsum(
        "thd,hde->the", query_float, incoming, precision=HIGH
    )
    attended = local_out + inherited
    hidden = normalize(attended, norm_gain, gate_logits)
    weight_rows = lax.all_gather(out_weight, ("chip", "core"), axis=1, tiled=True)
    pieces = []
    for rows in jnp.split(hidden, 2, axis=0):
        terms = jnp.dot(rows, weight_rows, preferred_element_type=jnp.float32)
        pieces.append(lax.psum_scatter(terms, "tensor", scatter_dimension=1, tiled=True))
    mixed = jnp.concatenate(pieces, axis=0)
    return mixed


def solution(mesh):
    seq_len, groups = mesh.devices.shape
    split = Mesh(mesh.devices.reshape(seq_len // 2, 2, groups), ("chip", "core", "tensor"))
    tokens = ("chip", "core")
    return jax.shard_map(
        per_device,
        mesh=split,
        in_specs=(
            P(tokens, "tensor"),
            P(tokens, "tensor"),
            P(tokens, "tensor"),
            P(tokens, "tensor"),
            P(tokens, "tensor"),
            P("tensor", None, None),
            P("tensor"),
            P("tensor", tokens),
        ),
        out_specs=P(tokens, "tensor"),
        check_vma=False,
    )
```

```python
import jax
import jax.numpy as jnp
from jax import lax
from jax.sharding import Mesh, PartitionSpec as P

HIGH = lax.Precision.HIGHEST


def entering(array, axis, combine, identity):
    length, mine = (lax.axis_size(axis), lax.axis_index(axis))
    everything = jax.tree.map(lambda part: lax.all_gather(part, axis), array)
    start = jax.tree.map(
        lambda part, zero: jnp.broadcast_to(jnp.asarray(zero, part.dtype), part.shape),
        array,
        identity,
    )

    def hop(k, before):
        reached = k < mine
        new = combine(before, jax.tree.map(lambda part: part[k], everything))
        return jax.tree.map(lambda a, b: jnp.where(reached, a, b), new, before)

    return lax.fori_loop(0, length, hop, start)


def block_step(state, pieces):
    queries_b, keys_b, values_b, decay_b = pieces
    cumulative_memory = jnp.cumsum(decay_b, axis=0)
    total = cumulative_memory[-1]
    carried = jnp.exp(cumulative_memory)[:, :, None] * jnp.einsum(
        "thd,hde->the", queries_b.astype(jnp.float32), state, precision=HIGH
    )
    scores = jnp.einsum("thd,shd->hts", queries_b, keys_b, preferred_element_type=jnp.float32)
    length = cumulative_memory.shape[0]
    lower = jnp.tril(jnp.ones((length, length), dtype=bool))[None]
    spread = cumulative_memory.T[:, :, None] - cumulative_memory.T[:, None, :]
    weights = jnp.where(lower, jnp.exp(jnp.where(lower, spread, 0.0)), 0.0)
    mixes = (scores * weights).astype(jnp.bfloat16)
    local = jnp.einsum("hts,she->the", mixes, values_b, preferred_element_type=jnp.float32)
    scaled = keys_b.astype(jnp.float32) * jnp.exp(total[None, :] - cumulative_memory)[:, :, None]
    new_state = jnp.exp(total)[:, None, None] * state + jnp.einsum(
        "shd,she->hde", scaled, values_b.astype(jnp.float32), precision=HIGH
    )
    return (new_state, carried + local)


def normalize(attended, norm_gain, gate_logits):
    mean_square = jnp.mean(attended * attended, axis=-1, keepdims=True)
    normalized_output = attended * lax.rsqrt(mean_square + 1e-05)
    flat = normalized_output.reshape(attended.shape[0], -1)
    gated = flat * norm_gain[None, :] * jax.nn.sigmoid(gate_logits.astype(jnp.float32))
    return gated.astype(jnp.bfloat16)


def chain_link(earlier, later):
    return (earlier[0] * later[0], later[0][:, None, None] * earlier[1] + later[1])


def pack(rates, state):
    heads = state.shape[0]
    flat = state.reshape(heads, -1)
    lanes = jnp.broadcast_to(rates[:, None], (heads, 128))
    return jnp.concatenate([flat, lanes], axis=1)


def link_packed(earlier, later):
    width = later.shape[1] - 128
    later_rate = later[:, width:width + 1]
    state = later_rate * earlier[:, :width] + later[:, :width]
    rate = earlier[:, width:] * later[:, width:]
    return jnp.concatenate([state, rate], axis=1)


def swap_cores(array):
    return lax.ppermute(array, "core", [(0, 1), (1, 0)])


def carried_in(rates, state, initial_state):
    chips, chip = (lax.axis_size("chip"), lax.axis_index("chip"))
    core = lax.axis_index("core")
    half = state.shape[0] // 2
    own = pack(rates, state)
    own_mine = lax.dynamic_slice_in_dim(own, core * half, half, axis=0)
    own_other = lax.dynamic_slice_in_dim(own, (1 - core) * half, half, axis=0)
    partner_mine = swap_cores(own_other)
    first_core = jnp.where(core == 0, own_mine, partner_mine)
    second_core = jnp.where(core == 0, partner_mine, own_mine)
    chip_element = link_packed(first_core, second_core)
    identity = pack(jnp.ones((half,), rates.dtype), jnp.zeros_like(state[:half]))
    before = identity
    through = chip_element
    step = 1
    while step < chips:
        received = [
            lax.ppermute(through, "chip", [(i, i + m * step) for i in range(chips - m * step)])
            for m in range(1, 4)
            if m * step < chips
        ]
        for m, earlier in enumerate(received, start=1):
            before = jnp.where(chip >= m * step, link_packed(earlier, before), before)
        through = link_packed(before, chip_element)
        step *= 4
    start_state = lax.dynamic_slice_in_dim(initial_state, core * half, half, axis=0)
    first = pack(jnp.ones((half,), rates.dtype), start_state)
    current = link_packed(first, before)
    for_second = link_packed(current, first_core)
    keep = jnp.where(core == 0, current, for_second)
    other = swap_cores(jnp.where(core == 0, for_second, current))
    whole = jnp.where(core == 0, jnp.concatenate([keep, other]), jnp.concatenate([other, keep]))
    width = whole.shape[1] - 128
    return whole[:, :width].reshape(state.shape)


def per_device(
    queries, key_vectors, value_rows, gate_logits, log_decay, initial_state, norm_gain, out_weight
):
    rows_here = queries.shape[0]
    head_count = log_decay.shape[1]
    head_dim = initial_state.shape[1]
    block_len = min(512, rows_here)
    block_count = rows_here // block_len

    def shaped(array):
        return array.reshape(block_count, block_len, head_count, head_dim)

    zero_state = jnp.zeros((head_count, head_dim, head_dim), jnp.float32)
    decay_blocks = log_decay.reshape(block_count, block_len, head_count)
    device_state, outputs = lax.scan(
        block_step,
        zero_state,
        (shaped(queries), shaped(key_vectors), shaped(value_rows), decay_blocks),
    )
    local_out = outputs.reshape(rows_here, head_count, head_dim)
    through = jnp.cumsum(log_decay, axis=0)
    shard_fading_rates = jnp.exp(through[-1])
    incoming = carried_in(shard_fading_rates, device_state, initial_state)
    query_float = queries.reshape(rows_here, head_count, head_dim).astype(jnp.float32)
    inherited = jnp.exp(through)[:, :, None] * jnp.einsum(
        "thd,hde->the", query_float, incoming, precision=HIGH
    )
    attended = local_out + inherited
    hidden = normalize(attended, norm_gain, gate_logits)
    terms = jnp.dot(
        hidden,
        lax.all_gather(out_weight, ("chip", "core"), axis=1, tiled=True),
        preferred_element_type=jnp.float32,
    )
    mixed = lax.psum_scatter(terms, "tensor", scatter_dimension=1, tiled=True)
    return mixed


def solution(mesh):
    seq_len, groups = mesh.devices.shape
    split = Mesh(mesh.devices.reshape(seq_len // 2, 2, groups), ("chip", "core", "tensor"))
    tokens = ("chip", "core")
    return jax.shard_map(
        per_device,
        mesh=split,
        in_specs=(
            P(tokens, "tensor"),
            P(tokens, "tensor"),
            P(tokens, "tensor"),
            P(tokens, "tensor"),
            P(tokens, "tensor"),
            P("tensor", None, None),
            P("tensor"),
            P("tensor", tokens),
        ),
        out_specs=P(tokens, "tensor"),
        check_vma=False,
    )
```

```python
import jax
import jax.numpy as jnp
from jax import lax
from jax.sharding import Mesh, PartitionSpec as P

HIGH = lax.Precision.HIGHEST


def entering(array, axis, combine, identity):
    length, mine = (lax.axis_size(axis), lax.axis_index(axis))
    everything = jax.tree.map(lambda part: lax.all_gather(part, axis), array)
    start = jax.tree.map(
        lambda part, zero: jnp.broadcast_to(jnp.asarray(zero, part.dtype), part.shape),
        array,
        identity,
    )

    def hop(k, before):
        reached = k < mine
        new = combine(before, jax.tree.map(lambda part: part[k], everything))
        return jax.tree.map(lambda a, b: jnp.where(reached, a, b), new, before)

    return lax.fori_loop(0, length, hop, start)


def block_step(state, pieces):
    queries_b, keys_b, values_b, decay_b = pieces
    cumulative_memory = jnp.cumsum(decay_b, axis=0)
    total = cumulative_memory[-1]
    carried = jnp.exp(cumulative_memory)[:, :, None] * jnp.einsum(
        "thd,hde->the", queries_b.astype(jnp.float32), state, precision=HIGH
    )
    scores = jnp.einsum("thd,shd->hts", queries_b, keys_b, preferred_element_type=jnp.float32)
    length = cumulative_memory.shape[0]
    lower = jnp.tril(jnp.ones((length, length), dtype=bool))[None]
    spread = cumulative_memory.T[:, :, None] - cumulative_memory.T[:, None, :]
    weights = jnp.where(lower, jnp.exp(jnp.where(lower, spread, 0.0)), 0.0)
    mixes = (scores * weights).astype(jnp.bfloat16)
    local = jnp.einsum("hts,she->the", mixes, values_b, preferred_element_type=jnp.float32)
    scaled = keys_b.astype(jnp.float32) * jnp.exp(total[None, :] - cumulative_memory)[:, :, None]
    new_state = jnp.exp(total)[:, None, None] * state + jnp.einsum(
        "shd,she->hde", scaled, values_b.astype(jnp.float32), precision=HIGH
    )
    return (new_state, carried + local)


def normalize(attended, norm_gain, gate_logits):
    mean_square = jnp.mean(attended * attended, axis=-1, keepdims=True)
    normalized_output = attended * lax.rsqrt(mean_square + 1e-05)
    flat = normalized_output.reshape(attended.shape[0], -1)
    gated = flat * norm_gain[None, :] * jax.nn.sigmoid(gate_logits.astype(jnp.float32))
    return gated.astype(jnp.bfloat16)


def chain_link(earlier, later):
    return (earlier[0] * later[0], later[0][:, None, None] * earlier[1] + later[1])


def pack(rates, state):
    heads = state.shape[0]
    flat = state.reshape(heads, -1)
    lanes = jnp.broadcast_to(rates[:, None], (heads, 128))
    return jnp.concatenate([flat, lanes], axis=1)


def link_packed(earlier, later):
    width = later.shape[1] - 128
    later_rate = later[:, width:width + 1]
    state = later_rate * earlier[:, :width] + later[:, :width]
    rate = earlier[:, width:] * later[:, width:]
    return jnp.concatenate([state, rate], axis=1)


def swap_cores(array):
    return lax.ppermute(array, "core", [(0, 1), (1, 0)])


def carried_in(rates, state, initial_state):
    chips, chip = (lax.axis_size("chip"), lax.axis_index("chip"))
    core = lax.axis_index("core")
    half = state.shape[0] // 2
    own = pack(rates, state)
    own_mine = lax.dynamic_slice_in_dim(own, core * half, half, axis=0)
    own_other = lax.dynamic_slice_in_dim(own, (1 - core) * half, half, axis=0)
    partner_mine = swap_cores(own_other)
    first_core = jnp.where(core == 0, own_mine, partner_mine)
    second_core = jnp.where(core == 0, partner_mine, own_mine)
    chip_element = link_packed(first_core, second_core)
    identity = pack(jnp.ones((half,), rates.dtype), jnp.zeros_like(state[:half]))
    before = identity
    through = chip_element
    step = 1
    while step < chips:
        received = [
            lax.ppermute(through, "chip", [(i, i + m * step) for i in range(chips - m * step)])
            for m in range(1, 2)
            if m * step < chips
        ]
        for m, earlier in enumerate(received, start=1):
            before = jnp.where(chip >= m * step, link_packed(earlier, before), before)
        through = link_packed(before, chip_element)
        step *= 2
    start_state = lax.dynamic_slice_in_dim(initial_state, core * half, half, axis=0)
    first = pack(jnp.ones((half,), rates.dtype), start_state)
    current = link_packed(first, before)
    for_second = link_packed(current, first_core)
    keep = jnp.where(core == 0, current, for_second)
    other = swap_cores(jnp.where(core == 0, for_second, current))
    whole = jnp.where(core == 0, jnp.concatenate([keep, other]), jnp.concatenate([other, keep]))
    width = whole.shape[1] - 128
    return whole[:, :width].reshape(state.shape)


def per_device(
    queries, key_vectors, value_rows, gate_logits, log_decay, initial_state, norm_gain, out_weight
):
    rows_here = queries.shape[0]
    head_count = log_decay.shape[1]
    head_dim = initial_state.shape[1]
    block_len = min(512, rows_here)
    block_count = rows_here // block_len

    def shaped(array):
        return array.reshape(block_count, block_len, head_count, head_dim)

    zero_state = jnp.zeros((head_count, head_dim, head_dim), jnp.float32)
    decay_blocks = log_decay.reshape(block_count, block_len, head_count)
    device_state, outputs = lax.scan(
        block_step,
        zero_state,
        (shaped(queries), shaped(key_vectors), shaped(value_rows), decay_blocks),
    )
    local_out = outputs.reshape(rows_here, head_count, head_dim)
    through = jnp.cumsum(log_decay, axis=0)
    shard_fading_rates = jnp.exp(through[-1])
    incoming = carried_in(shard_fading_rates, device_state, initial_state)
    query_float = queries.reshape(rows_here, head_count, head_dim).astype(jnp.float32)
    inherited = jnp.exp(through)[:, :, None] * jnp.einsum(
        "thd,hde->the", query_float, incoming, precision=HIGH
    )
    attended = local_out + inherited
    hidden = normalize(attended, norm_gain, gate_logits)
    terms = jnp.dot(
        hidden,
        lax.all_gather(out_weight, ("chip", "core"), axis=1, tiled=True),
        preferred_element_type=jnp.float32,
    )
    mixed = lax.psum_scatter(terms, "tensor", scatter_dimension=1, tiled=True)
    return mixed


def solution(mesh):
    seq_len, groups = mesh.devices.shape
    split = Mesh(mesh.devices.reshape(seq_len // 2, 2, groups), ("chip", "core", "tensor"))
    tokens = ("chip", "core")
    return jax.shard_map(
        per_device,
        mesh=split,
        in_specs=(
            P(tokens, "tensor"),
            P(tokens, "tensor"),
            P(tokens, "tensor"),
            P(tokens, "tensor"),
            P(tokens, "tensor"),
            P("tensor", None, None),
            P("tensor"),
            P("tensor", tokens),
        ),
        out_specs=P(tokens, "tensor"),
        check_vma=False,
    )
```

```python
import jax
import jax.numpy as jnp
from jax import lax
from jax.sharding import Mesh, PartitionSpec as P

HIGH = lax.Precision.HIGHEST


def entering(array, axis, combine, identity):
    length, mine = (lax.axis_size(axis), lax.axis_index(axis))
    everything = jax.tree.map(lambda part: lax.all_gather(part, axis), array)
    start = jax.tree.map(
        lambda part, zero: jnp.broadcast_to(jnp.asarray(zero, part.dtype), part.shape),
        array,
        identity,
    )

    def hop(k, before):
        reached = k < mine
        new = combine(before, jax.tree.map(lambda part: part[k], everything))
        return jax.tree.map(lambda a, b: jnp.where(reached, a, b), new, before)

    return lax.fori_loop(0, length, hop, start)


def block_step(state, pieces):
    queries_b, keys_b, values_b, decay_b = pieces
    cumulative_memory = jnp.cumsum(decay_b, axis=0)
    total = cumulative_memory[-1]
    carried = jnp.exp(cumulative_memory)[:, :, None] * jnp.einsum(
        "thd,hde->the", queries_b.astype(jnp.float32), state, precision=HIGH
    )
    scores = jnp.einsum("thd,shd->hts", queries_b, keys_b, preferred_element_type=jnp.float32)
    length = cumulative_memory.shape[0]
    lower = jnp.tril(jnp.ones((length, length), dtype=bool))[None]
    spread = cumulative_memory.T[:, :, None] - cumulative_memory.T[:, None, :]
    weights = jnp.where(lower, jnp.exp(jnp.where(lower, spread, 0.0)), 0.0)
    mixes = (scores * weights).astype(jnp.bfloat16)
    local = jnp.einsum("hts,she->the", mixes, values_b, preferred_element_type=jnp.float32)
    scaled = keys_b.astype(jnp.float32) * jnp.exp(total[None, :] - cumulative_memory)[:, :, None]
    new_state = jnp.exp(total)[:, None, None] * state + jnp.einsum(
        "shd,she->hde", scaled, values_b.astype(jnp.float32), precision=HIGH
    )
    return (new_state, carried + local)


def normalize(attended, norm_gain, gate_logits):
    mean_square = jnp.mean(attended * attended, axis=-1, keepdims=True)
    normalized_output = attended * lax.rsqrt(mean_square + 1e-05)
    flat = normalized_output.reshape(attended.shape[0], -1)
    gated = flat * norm_gain[None, :] * jax.nn.sigmoid(gate_logits.astype(jnp.float32))
    return gated.astype(jnp.bfloat16)


def chain_link(earlier, later):
    return (earlier[0] * later[0], later[0][:, None, None] * earlier[1] + later[1])


def pack(rates, state):
    heads = state.shape[0]
    flat = state.reshape(heads, -1)
    lanes = jnp.broadcast_to(rates[:, None], (heads, 128))
    return jnp.concatenate([flat, lanes], axis=1)


def link_packed(earlier, later):
    width = later.shape[1] - 128
    later_rate = later[:, width:width + 1]
    state = later_rate * earlier[:, :width] + later[:, :width]
    rate = earlier[:, width:] * later[:, width:]
    return jnp.concatenate([state, rate], axis=1)


def swap_cores(array):
    return lax.ppermute(array, "core", [(0, 1), (1, 0)])


def carried_in(rates, state, initial_state):
    chips, chip = (lax.axis_size("chip"), lax.axis_index("chip"))
    core = lax.axis_index("core")
    half = state.shape[0] // 2
    own = pack(rates, state)
    own_mine = lax.dynamic_slice_in_dim(own, core * half, half, axis=0)
    own_other = lax.dynamic_slice_in_dim(own, (1 - core) * half, half, axis=0)
    partner_mine = swap_cores(own_other)
    first_core = jnp.where(core == 0, own_mine, partner_mine)
    second_core = jnp.where(core == 0, partner_mine, own_mine)
    chip_element = link_packed(first_core, second_core)
    identity = pack(jnp.ones((half,), rates.dtype), jnp.zeros_like(state[:half]))
    before = identity
    through = chip_element
    step = 1
    while step < chips:
        received = [
            lax.ppermute(through, "chip", [(i, i + m * step) for i in range(chips - m * step)])
            for m in range(1, 2)
            if m * step < chips
        ]
        for m, earlier in enumerate(received, start=1):
            before = jnp.where(chip >= m * step, link_packed(earlier, before), before)
        through = link_packed(before, chip_element)
        step *= 2
    start_state = lax.dynamic_slice_in_dim(initial_state, core * half, half, axis=0)
    first = pack(jnp.ones((half,), rates.dtype), start_state)
    current = link_packed(first, before)
    for_second = link_packed(current, first_core)
    keep = jnp.where(core == 0, current, for_second)
    other = swap_cores(jnp.where(core == 0, for_second, current))
    whole = jnp.where(core == 0, jnp.concatenate([keep, other]), jnp.concatenate([other, keep]))
    width = whole.shape[1] - 128
    return whole[:, :width].reshape(state.shape)


def per_device(
    queries, key_vectors, value_rows, gate_logits, log_decay, initial_state, norm_gain, out_weight
):
    rows_here = queries.shape[0]
    head_count = log_decay.shape[1]
    head_dim = initial_state.shape[1]
    block_len = min(512, rows_here)
    block_count = rows_here // block_len

    def shaped(array):
        return array.reshape(block_count, block_len, head_count, head_dim)

    zero_state = jnp.zeros((head_count, head_dim, head_dim), jnp.float32)
    decay_blocks = log_decay.reshape(block_count, block_len, head_count)
    device_state, outputs = lax.scan(
        block_step,
        zero_state,
        (shaped(queries), shaped(key_vectors), shaped(value_rows), decay_blocks),
    )
    local_out = outputs.reshape(rows_here, head_count, head_dim)
    through = jnp.cumsum(log_decay, axis=0)
    shard_fading_rates = jnp.exp(through[-1])
    incoming = carried_in(shard_fading_rates, device_state, initial_state)
    query_float = queries.reshape(rows_here, head_count, head_dim).astype(jnp.float32)
    inherited = jnp.exp(through)[:, :, None] * jnp.einsum(
        "thd,hde->the", query_float, incoming, precision=HIGH
    )
    attended = local_out + inherited
    hidden = normalize(attended, norm_gain, gate_logits)
    width = out_weight.shape[1] // 2
    halves = []
    for part in (out_weight[:, :width], out_weight[:, width:]):
        gathered = lax.all_gather(part, ("chip", "core"), axis=1, tiled=True)
        product = jnp.dot(hidden, gathered, preferred_element_type=jnp.float32)
        halves.append(product.reshape(rows_here, -1, width))
    terms = jnp.concatenate(halves, axis=2).reshape(rows_here, -1)
    mixed = lax.psum_scatter(terms, "tensor", scatter_dimension=1, tiled=True)
    return mixed


def solution(mesh):
    seq_len, groups = mesh.devices.shape
    split = Mesh(mesh.devices.reshape(seq_len // 2, 2, groups), ("chip", "core", "tensor"))
    tokens = ("chip", "core")
    return jax.shard_map(
        per_device,
        mesh=split,
        in_specs=(
            P(tokens, "tensor"),
            P(tokens, "tensor"),
            P(tokens, "tensor"),
            P(tokens, "tensor"),
            P(tokens, "tensor"),
            P("tensor", None, None),
            P("tensor"),
            P("tensor", tokens),
        ),
        out_specs=P(tokens, "tensor"),
        check_vma=False,
    )
```
